32 devices in a mesh: parts: 2 (over y), set: 4 (over x, core), seq: 4 (over z).
Axes of the slice: x: 2, y: 2, z: 4, core: 2. Of those that a mesh axis runs over, the one named last changes fastest.
Arguments:
- span_hidden: bfloat16 [512, 8192], P('parts', 'seq'), parts along dimension 0, may hold values from -500 to 500
- norm_gain: bfloat16 [8192], P('seq'), may hold values from 0.099609375 to 1.8984375
- key_value_weight: bfloat16 [8192, 2048], P('seq', 'set'), may hold values from -0.0625 to 0.0625
- prompt_key_value: bfloat16 [256, 2048], P(('parts', 'seq')), parts along dimension 0, may hold values from -6 to 6
- span_offset: int32 [2], P('parts'), parts along dimension 0, may hold values from 64 to 128
- cont_query: bfloat16 [32, 64, 8192], P(('parts', 'set', 'seq')), parts along dimension 0, may hold values from -24 to 24
- continuation_key_value: bfloat16 [32, 64, 2048], P(('parts', 'set', 'seq')), parts along dimension 0, may hold values from -6 to 6
- cont_lengths: int32 [32], P(('parts', 'set', 'seq')), parts along dimension 0, may hold values from 1 to 64
Outputs:
- span_key_value: bfloat16 [512, 2048], P(('parts', 'seq'), 'set'), parts along dimension 0
- attended: bfloat16 [32, 64, 8192], P(('parts', 'set', 'seq')), parts along dimension 0
The draws below stay inside these ranges and needn't reach their ends.
There are 2 independent parts, one for each index of `parts`. The reference program is written for one: setup_inputs(seed, part) draws one part's arguments, and reference() takes and returns one part's arrays. A program takes and returns all parts, laid end to end along the dimension named above; an argument that names none is the same for every part. Nothing has to cross between parts.
All inputs are finite; a program needn't handle non-finite values.
Results may differ from the reference program's by a relative error of at most 0.02.
Values may be sent and summed in bfloat16 or wider, within the bound.
A program may use at most 64 MiB of HBM per device.

```python
import math
import jax
import jax.numpy as jnp
from jax import lax

MODEL_WIDTH = 8192
QUERY_HEADS = 64
KEY_HEADS = 8
HEAD_SIZE = 128
SPAN_LENGTH = 256
CONTINUE_LENGTH = 64
PROMPT_LENGTH = 128
CONTINUATION_SET = 16


def draw_span_hidden(key, part):
    first, second = jax.random.split(jax.random.fold_in(key, 11), 2)
    columns = jnp.arange(MODEL_WIDTH).astype(jnp.float32) / MODEL_WIDTH
    ramp = 0.6 * 3.0 ** columns
    rough = jax.random.uniform(second, (MODEL_WIDTH,), jnp.float32, 0.5, 1.5)
    base = jnp.clip(jax.random.normal(first, (SPAN_LENGTH, MODEL_WIDTH), jnp.float32), -6.0, 6.0)
    result = base * (ramp * rough)[None, :]
    return result.astype(jnp.bfloat16)


def continuation_pair(key):
    query_key, kv_key = jax.random.split(jax.random.fold_in(key, 23), 2)
    key_value_shape = (CONTINUATION_SET, CONTINUE_LENGTH, 2 * KEY_HEADS * HEAD_SIZE)
    query_shape = (CONTINUATION_SET, CONTINUE_LENGTH, QUERY_HEADS * HEAD_SIZE)
    key_value_sample = jnp.clip(jax.random.normal(kv_key, key_value_shape, jnp.float32), -6.0, 6.0)
    query_draw = jnp.clip(jax.random.normal(query_key, query_shape, jnp.float32), -6.0, 6.0)
    return (query_draw, key_value_sample)


def draw_cont_query(key, part):
    return continuation_pair(key)[0].astype(jnp.bfloat16)


def draw_continuation_key_value(key, part):
    return continuation_pair(key)[1].astype(jnp.bfloat16)


def place_ends(drawn, stream_key, least, high):
    spot = [jax.random.randint(jax.random.fold_in(stream_key, axis), (), 0, length) for axis, length in enumerate(drawn.shape)]
    main_axis = drawn.shape.index(max(drawn.shape))
    next_to = spot[:main_axis] + [(spot[main_axis] + 1) % drawn.shape[main_axis]] + spot[main_axis + 1:]
    return drawn.at[tuple(spot)].set(least).at[tuple(next_to)].set(high)


def block_scale(stream_key, dims, cuts, least, largest):
    def one(position, blocks):
        draws = jax.random.uniform(jax.random.fold_in(jax.random.fold_in(stream_key, 6), position), (blocks,), jnp.float32, least / len(cuts), largest / len(cuts))
        return jnp.repeat(jnp.exp(draws), dims[position] // blocks).reshape((-1,) + (1,) * (len(dims) - position - 1))

    loudness = one(*cuts[0])
    for cut in cuts[1:]:
        loudness = loudness * one(*cut)
    return loudness


def bell_draw(stream_key, shape, spread, most, pieces=(), kind=jnp.bfloat16):
    loudness = block_scale(stream_key, shape, pieces, -0.22, 0.18) if pieces else 1.0
    entries = jax.random.normal(stream_key, shape, jnp.float32) * spread * loudness
    return jnp.minimum(jnp.maximum(entries, -most), most).astype(kind)


def setup_inputs(seed: int = 0, part: int = 0) -> dict:
    streams_of = jax.random.split(jax.random.key(seed), 9)
    own_keys = jax.random.split(jax.random.fold_in(streams_of[8], part), 9)
    span_hidden = draw_span_hidden(jax.random.fold_in(jax.random.fold_in(streams_of[8], part), 71), part)
    norm_gain = jnp.clip(1.0 + 0.18 * jax.random.normal(streams_of[1], (MODEL_WIDTH,), jnp.float32), 0.099609375, 1.8984375).astype(jnp.bfloat16)
    key_value_weight = bell_draw(streams_of[2], (MODEL_WIDTH, 2 * KEY_HEADS * HEAD_SIZE), MODEL_WIDTH ** -0.5, 0.0625, ((0, 4), (1, 4)))
    prompt_key_value = bell_draw(own_keys[3], (PROMPT_LENGTH, 2 * KEY_HEADS * HEAD_SIZE), 1.0, 6.0, ((0, 4),))
    span_offset = jax.random.randint(own_keys[4], (1,), PROMPT_LENGTH // 2, PROMPT_LENGTH + 1).astype(jnp.int32)
    cont_query = draw_cont_query(jax.random.fold_in(jax.random.fold_in(streams_of[8], part), 71), part)
    continuation_key_value = draw_continuation_key_value(jax.random.fold_in(jax.random.fold_in(streams_of[8], part), 71), part)
    cont_lengths = place_ends(jax.random.randint(own_keys[7], (CONTINUATION_SET,), 1, CONTINUE_LENGTH + 1), jax.random.fold_in(own_keys[7], 1), 1, CONTINUE_LENGTH).astype(jnp.int32)
    return dict(span_hidden=span_hidden, norm_gain=norm_gain, key_value_weight=key_value_weight, prompt_key_value=prompt_key_value, span_offset=span_offset, cont_query=cont_query, continuation_key_value=continuation_key_value, cont_lengths=cont_lengths)


EPS = 1e-05
NEGATIVE_LARGE = -1e+30

def frequencies(count, width, dtype):
    base = 500000.0 ** (-(jnp.arange(count).astype(dtype) * 2.0) / width)
    wave = 2.0 * math.pi / base
    smooth = (8192.0 / wave - 1.0) / 3.0
    blended = (1.0 - smooth) * base / 8.0 + smooth * base
    return jnp.where(wave < 2048.0, base, jnp.where(wave > 8192.0, base / 8.0, blended))

def apply_rotary(value_matrix, positions):
    mid_point = value_matrix.shape[-1] // 2
    frequency = frequencies(mid_point, value_matrix.shape[-1], value_matrix.dtype)
    angles = positions.astype(value_matrix.dtype)[:, None] * frequency[None, :]
    cosine = jnp.concatenate([jnp.cos(angles), jnp.cos(angles)], -1)[:, None, :]
    sine_part = jnp.concatenate([jnp.sin(angles), jnp.sin(angles)], -1)[:, None, :]
    turned = jnp.concatenate([-value_matrix[..., mid_point:], value_matrix[..., :mid_point]], -1)
    return value_matrix * cosine + turned * sine_part

def reference(span_hidden, norm_gain, key_value_weight, prompt_key_value, span_offset, cont_query, continuation_key_value, cont_lengths):
    key_columns_width = KEY_HEADS * HEAD_SIZE
    group_factor = QUERY_HEADS // KEY_HEADS
    hidden = span_hidden.astype(jnp.float32)
    mean_square = lax.optimization_barrier(jnp.sum(hidden * hidden, axis=1)) / MODEL_WIDTH
    normed = (hidden * lax.rsqrt(mean_square + EPS)[:, None] * norm_gain.astype(jnp.float32)[None, :]).astype(jnp.bfloat16)
    projected_rows = jnp.dot(normed, key_value_weight, preferred_element_type=jnp.float32)
    offset = span_offset[0]
    span_positions = offset + jnp.arange(SPAN_LENGTH, dtype=jnp.int32)
    rotary_applied = apply_rotary(projected_rows[:, :key_columns_width].reshape(SPAN_LENGTH, KEY_HEADS, HEAD_SIZE), span_positions).reshape(SPAN_LENGTH, key_columns_width)
    span_key_value = jnp.concatenate([rotary_applied, projected_rows[:, key_columns_width:]], 1).astype(jnp.bfloat16)
    prior_key_rows = jnp.concatenate([prompt_key_value[:, :key_columns_width], span_key_value[:, :key_columns_width]], 0).reshape(PROMPT_LENGTH + SPAN_LENGTH, KEY_HEADS, HEAD_SIZE)
    prior_value_rows = jnp.concatenate([prompt_key_value[:, key_columns_width:], span_key_value[:, key_columns_width:]], 0).reshape(PROMPT_LENGTH + SPAN_LENGTH, KEY_HEADS, HEAD_SIZE)
    past_valid = jnp.concatenate([jnp.arange(PROMPT_LENGTH, dtype=jnp.int32) < offset, jnp.ones((SPAN_LENGTH,), bool)])
    self_positions = offset + SPAN_LENGTH + jnp.arange(CONTINUE_LENGTH, dtype=jnp.int32)
    token_index = jnp.arange(CONTINUE_LENGTH, dtype=jnp.int32)
    causal = token_index[:, None] >= token_index[None, :]
    valid = jnp.concatenate([jnp.broadcast_to(past_valid[None, :], (CONTINUE_LENGTH, PROMPT_LENGTH + SPAN_LENGTH)), causal], 1)
    valid_four = valid[:, None, None, :]

    def score_one(item):
        query_raw, key_value_plain, sequence_length = item
        query_rows = apply_rotary(query_raw.astype(jnp.float32).reshape(CONTINUE_LENGTH, QUERY_HEADS, HEAD_SIZE), self_positions).astype(jnp.bfloat16)
        query_rows = query_rows.reshape(CONTINUE_LENGTH, KEY_HEADS, group_factor, HEAD_SIZE)
        self_key_rows = apply_rotary(key_value_plain[:, :key_columns_width].astype(jnp.float32).reshape(CONTINUE_LENGTH, KEY_HEADS, HEAD_SIZE), self_positions).astype(jnp.bfloat16)
        self_value_rows = key_value_plain[:, key_columns_width:].reshape(CONTINUE_LENGTH, KEY_HEADS, HEAD_SIZE)
        key_matrix = jnp.concatenate([prior_key_rows, self_key_rows], 0).astype(jnp.float32)
        vals = jnp.concatenate([prior_value_rows, self_value_rows], 0).astype(jnp.float32)
        scores = jnp.einsum('tgkd,ngd->tgkn', query_rows.astype(jnp.float32), key_matrix) * HEAD_SIZE ** (-0.5)
        masked = jnp.where(valid_four, scores, NEGATIVE_LARGE)
        top = lax.optimization_barrier(jnp.max(masked, axis=-1))
        weights = jnp.where(valid_four, jnp.exp(masked - top[..., None]), 0.0)
        total = lax.optimization_barrier(jnp.sum(weights, axis=-1))
        rounded = weights.astype(jnp.bfloat16).astype(jnp.float32)
        mixed = jnp.einsum('tgkn,ngd->tgkd', rounded, vals) / total[..., None]
        mixed = mixed.reshape(CONTINUE_LENGTH, QUERY_HEADS * HEAD_SIZE)
        live = token_index < sequence_length
        return jnp.where(live[:, None], mixed, 0.0).astype(jnp.bfloat16)
    attended = lax.map(score_one, (cont_query, continuation_key_value, cont_lengths))
    return (span_key_value, attended)
```

```python
import functools
import math

import jax
import jax.numpy as jnp
import numpy as np
from jax import lax
from jax.experimental import pallas as pl
from jax.experimental.pallas import tpu as pltpu
from jax.sharding import PartitionSpec as P

MODEL_WIDTH = 8192
QUERY_HEADS = 64
KEY_HEADS = 8
HEAD_SIZE = 128
SPAN_LENGTH = 256
GROUP = QUERY_HEADS // KEY_HEADS
KEY_COLUMNS = KEY_HEADS * HEAD_SIZE

EPS = 1e-05
NEGATIVE_LARGE = -1e30
EXPONENT = HEAD_SIZE ** (-0.5) * math.log2(math.e)

MESH = pl.DeviceIdType.MESH
F32 = jnp.float32
BF16 = jnp.bfloat16


def frequency_table():
    index = np.arange(HEAD_SIZE // 2, dtype=np.float64)
    base = 500000.0 ** (-2.0 * index / HEAD_SIZE)
    wave = 2.0 * np.pi / base
    smooth = (8192.0 / wave - 1.0) / 3.0
    blended = (1.0 - smooth) * base / 8.0 + smooth * base
    table = np.where(wave < 2048.0, base, np.where(wave > 8192.0, base / 8.0, blended))
    row = np.concatenate([table, table]).astype(np.float32)
    return np.broadcast_to(row, (8, HEAD_SIZE)).copy()


def rotary_tables(frequency, start, rows):
    positions = (start + lax.broadcasted_iota(jnp.int32, (rows, HEAD_SIZE), 0)).astype(F32)
    angles = positions * frequency
    lane = lax.broadcasted_iota(jnp.int32, (rows, HEAD_SIZE), 1)
    sine = jnp.sin(angles)
    return jnp.cos(angles), jnp.where(lane < HEAD_SIZE // 2, -sine, sine)


def turn(value, cosine, sine):
    return value * cosine + pltpu.roll(value, HEAD_SIZE // 2, 1) * sine


def scores_of(query, keys):
    return lax.dot_general(query, keys, (((1,), (1,)), ((), ())), preferred_element_type=F32)


def with_ones(values):
    return jnp.concatenate([values, jnp.ones_like(values)], axis=1)


def kernel(
    n_set,
    n_seq,
    hidden_hbm,
    gain_hbm,
    weight_hbm,
    prompt_hbm,
    offset_smem,
    query_hbm,
    own_hbm,
    frequency_hbm,
    span_out,
    attended_out,
    hidden,
    gain,
    weight,
    prompt,
    query_in,
    own,
    frequency,
    scaled,
    partial,
    sending,
    received,
    square_mine,
    square_theirs,
    square_column,
    span,
    query,
    best,
    accum,
    load_sem,
    span_store_sem,
    square_send,
    square_recv,
    part_send,
    part_recv,
    pz_send,
    pz_recv,
    px_send,
    px_recv,
    pc_send,
    pc_recv,
    sz_send,
    sz_recv,
    sx_send,
    sx_recv,
    sc_send,
    sc_recv,
):
    n_x = n_set // 2
    me_set = lax.axis_index("set")
    me_seq = lax.axis_index("seq")
    me_x, me_core = me_set // 2, me_set % 2
    width = weight.shape[1]
    rows = span.shape[1] // n_seq
    cached = prompt.shape[1] // n_seq
    tokens = query_in.shape[0]
    halves = 2 if width % 512 == 0 else 1
    half = width // halves

    def seq_at(step):
        return (me_seq + step) % n_seq

    def set_at(step):
        return ((me_x + step) % n_x) * 2 + me_core

    twin = me_x * 2 + 1 - me_core

    def rows_of(which, count):
        return pl.ds(pl.multiple_of(which * count, count), count)

    loads = []

    def load(source, target):
        copy = pltpu.make_async_copy(source, target, load_sem.at[len(loads)])
        copy.start()
        loads.append(copy)
        return copy

    prompt_loads = [
        load(
            prompt_hbm.at[:, pl.ds(s * width, width)],
            prompt.at[s, rows_of(me_seq, cached), :],
        )
        for s in range(n_set)
    ]
    hidden_load = load(hidden_hbm, hidden)
    gain_load = load(gain_hbm, gain)
    weight_loads = [
        load(weight_hbm.at[:, pl.ds(i * half, half)], weight.at[:, pl.ds(i * half, half)])
        for i in range(halves)
    ]
    frequency_load = load(frequency_hbm, frequency)
    own_load = load(own_hbm.at[0], own)
    query_load = load(query_hbm.at[0], query_in)

    barrier = pltpu.get_barrier_semaphore()
    partners = [{"seq": seq_at(d)} for d in range(1, n_seq)]
    partners += [{"set": set_at(d)} for d in range(1, n_x)]
    partners += [{"set": twin}]
    for partner in partners:
        pl.semaphore_signal(barrier, inc=1, device_id=partner, device_id_type=MESH)

    hidden_load.wait()
    gain_load.wait()
    squares = jnp.zeros((hidden.shape[0], HEAD_SIZE), F32)
    for i in range(hidden.shape[1] // HEAD_SIZE):
        block = hidden[:, i * HEAD_SIZE : (i + 1) * HEAD_SIZE].astype(F32)
        squares += block * block
        scaled[:, i * HEAD_SIZE : (i + 1) * HEAD_SIZE] = (
            block * gain[i : i + 1, :].astype(F32)
        ).astype(BF16)
    square_row = jnp.sum(squares.T, axis=0, keepdims=True)
    square_mine[...] = jnp.broadcast_to(square_row, square_mine.shape)

    for copy in prompt_loads:
        copy.wait()
    pl.semaphore_wait(barrier, len(partners))

    copies = []

    def send(source, target, send_sem, recv_sem, device):
        copy = pltpu.make_async_remote_copy(
            src_ref=source,
            dst_ref=target,
            send_sem=send_sem,
            recv_sem=recv_sem,
            device_id=device,
            device_id_type=MESH,
        )
        copy.start()
        copies.append(copy)
        return copy

    def prompt_block(s, z):
        return prompt.at[s, rows_of(z, cached), :]

    def span_block(s, z):
        return span.at[s, rows_of(z, rows), :]

    prompt_z = []
    for d in range(1, n_seq):
        block = prompt_block(me_set, me_seq)
        prompt_z.append(
            send(block, block, pz_send.at[d], pz_recv.at[d], {"seq": seq_at(d)})
        )
    square_copies = [
        send(
            square_mine,
            square_theirs.at[d],
            square_send.at[d],
            square_recv.at[d],
            {"seq": seq_at(d)},
        )
        for d in range(1, n_seq)
    ]

    part_copies = []
    for i in range(halves):
        weight_loads[i].wait()
        columns = pl.ds(i * half, half)
        product = jnp.dot(scaled[...], weight[:, columns], preferred_element_type=F32)
        partial[:, columns] = product
        sending[i] = product.astype(BF16)
        for d in range(1, n_seq):
            part_copies.append(
                send(
                    sending.at[i, rows_of(seq_at(d), rows), :],
                    received.at[i, d],
                    part_send.at[i, d],
                    part_recv.at[i, d],
                    {"seq": seq_at(d)},
                )
            )

    frequency_load.wait()
    offset = offset_smem[0]
    cosine, sine = rotary_tables(frequency[0:1, :], offset + SPAN_LENGTH, tokens)
    span_cosine, span_sine = rotary_tables(frequency[0:1, :], offset + me_seq * rows, rows)
    own_load.wait()
    query_load.wait()

    causal = jnp.concatenate(
        [
            lax.broadcasted_iota(jnp.int32, (tokens, tokens), 0)
            >= lax.broadcasted_iota(jnp.int32, (tokens, tokens), 1)
        ]
        * GROUP,
        axis=0,
    )

    def columns_of(head):
        return pl.ds(pl.multiple_of(head * HEAD_SIZE, HEAD_SIZE), HEAD_SIZE)

    def attend_own(head, carry):
        for g in range(GROUP):
            raw = query_in[:, columns_of(head * GROUP + g)].astype(F32)
            query[head, pl.ds(g * tokens, tokens), :] = turn(raw, cosine, sine).astype(BF16)
        keys = turn(own[:, columns_of(head)].astype(F32), cosine, sine).astype(BF16)
        values = own[:, columns_of(head + KEY_HEADS)]
        scores = jnp.where(causal, scores_of(query[head], keys), NEGATIVE_LARGE)
        top = jnp.max(scores, axis=1, keepdims=True)
        weights = jnp.exp2((scores - top) * EXPONENT).astype(BF16)
        best[head] = jnp.broadcast_to(top, best.shape[1:])
        accum[head] = jnp.dot(weights, with_ones(values), preferred_element_type=F32)
        return carry

    def pass_prompt(d):
        prompt_z[d - 1].wait_recv()
        block = prompt_block(me_set, seq_at(n_seq - d))
        for e in range(1, n_x):
            send(block, block, px_send.at[d, e], px_recv.at[d, e], {"set": set_at(e)})
        send(block, block, pc_send.at[d, 0], pc_recv.at[d, 0], {"set": twin})

    def pass_prompt_twin(d):
        block = prompt_block(me_set, seq_at(n_seq - d))
        for e in range(1, n_x):
            pltpu.make_async_remote_copy(
                block, block, px_send.at[d, e], px_recv.at[d, e], {"set": set_at(e)}, MESH
            ).wait_recv()
            come = prompt_block(set_at(n_x - e), seq_at(n_seq - d))
            send(come, come, pc_send.at[d, e], pc_recv.at[d, e], {"set": twin})

    lax.fori_loop(0, KEY_HEADS // 4, attend_own, 0)
    for d in range(1, n_seq):
        pass_prompt(d)
    lax.fori_loop(KEY_HEADS // 4, KEY_HEADS, attend_own, 0)
    for d in range(1, n_seq):
        pass_prompt_twin(d)

    for copy in square_copies:
        copy.wait_recv()
    square_total = square_mine[...]
    for d in range(1, n_seq):
        square_total += square_theirs[d]
    square_column[...] = jnp.broadcast_to(
        square_total[0:1, :], (HEAD_SIZE, square_total.shape[1])
    ).T
    inverse = lax.rsqrt(square_column[rows_of(me_seq, rows), :] / MODEL_WIDTH + EPS)
    for copy in part_copies:
        copy.wait_recv()
    for i in range(halves):
        for j in range(half // HEAD_SIZE):
            column = i * half + j * HEAD_SIZE
            block = partial[rows_of(me_seq, rows), pl.ds(column, HEAD_SIZE)]
            for d in range(1, n_seq):
                block += received[i, d, :, pl.ds(j * HEAD_SIZE, HEAD_SIZE)].astype(F32)
            block = block * inverse
            turned = turn(block, span_cosine, span_sine)
            is_key = me_set * width + column < KEY_COLUMNS
            span[me_set, rows_of(me_seq, rows), pl.ds(column, HEAD_SIZE)] = jnp.where(
                is_key, turned, block
            ).astype(BF16)

    mine = span_block(me_set, me_seq)
    span_z = []
    sx, sc = {}, {}
    for e in range(1, n_x):
        sx[0, e] = send(mine, mine, sx_send.at[0, e], sx_recv.at[0, e], {"set": set_at(e)})
    for d in range(1, n_seq):
        span_z.append(send(mine, mine, sz_send.at[d], sz_recv.at[d], {"seq": seq_at(d)}))
    send(mine, mine, sc_send.at[0, 0], sc_recv.at[0, 0], {"set": twin})
    span_store = pltpu.make_async_copy(mine, span_out, span_store_sem)
    span_store.start()

    def pass_span(d):
        span_z[d - 1].wait_recv()
        block = span_block(me_set, seq_at(n_seq - d))
        for e in range(1, n_x):
            sx[d, e] = send(
                block, block, sx_send.at[d, e], sx_recv.at[d, e], {"set": set_at(e)}
            )
        send(block, block, sc_send.at[d, 0], sc_recv.at[d, 0], {"set": twin})

    def pass_span_twin(d):
        for e in range(1, n_x):
            sx[d, e].wait_recv()
            come = span_block(set_at(n_x - e), seq_at(n_seq - d))
            send(come, come, sc_send.at[d, e], sc_recv.at[d, e], {"set": twin})

    def attend_more(head, keys, values, mask):
        scores = scores_of(query[head], keys)
        if mask is not None:
            scores = jnp.where(mask, scores, NEGATIVE_LARGE)
        old = best[head][:, 0:1]
        top = jnp.maximum(old, jnp.max(scores, axis=1, keepdims=True))
        weights = jnp.exp2((scores - top) * EXPONENT).astype(BF16)
        shrink = jnp.exp2((old - top) * EXPONENT)
        total = accum[head] * shrink + jnp.dot(
            weights, with_ones(values), preferred_element_type=F32
        )
        return top, total

    per_set = width // HEAD_SIZE

    def head_of(array, head):
        return array[head // per_set, :, columns_of(head % per_set)]

    live = (
        lax.broadcasted_iota(jnp.int32, (1, prompt.shape[1]), 1) < offset
    )

    def attend_prompt(head, carry):
        top, total = attend_more(
            head, head_of(prompt, head), head_of(prompt, head + KEY_HEADS), live
        )
        best[head] = jnp.broadcast_to(top, best.shape[1:])
        accum[head] = total
        return carry

    for d in range(1, n_seq):
        for e in range(n_x):
            pltpu.make_async_remote_copy(
                prompt_block(me_set, me_seq),
                prompt_block(me_set, me_seq),
                pc_send.at[d, e],
                pc_recv.at[d, e],
                {"set": twin},
                MESH,
            ).wait_recv()
    cut = [KEY_HEADS * d // n_seq for d in range(n_seq + 1)]
    lax.fori_loop(cut[0], cut[1], attend_prompt, 0)
    pass_span_twin(0)
    for d in range(1, n_seq):
        pass_span(d)
        if cut[d] < cut[d + 1]:
            lax.fori_loop(cut[d], cut[d + 1], attend_prompt, 0)
    for d in range(1, n_seq):
        pass_span_twin(d)
    for d in range(n_seq):
        for e in range(n_x):
            pltpu.make_async_remote_copy(
                mine, mine, sc_send.at[d, e], sc_recv.at[d, e], {"set": twin}, MESH
            ).wait_recv()

    def attend_span(head, carry):
        top, total = attend_more(
            head, head_of(span, head), head_of(span, head + KEY_HEADS), None
        )
        mixed = (total[:, :HEAD_SIZE] / total[:, HEAD_SIZE:]).astype(BF16)
        for g in range(GROUP):
            attended_out[:, columns_of(head * GROUP + g)] = mixed[
                g * tokens : (g + 1) * tokens, :
            ]
        return carry

    lax.fori_loop(0, KEY_HEADS, attend_span, 0)

    for copy in copies:
        copy.wait_send()
    span_store.wait()


def on_device(
    n_set,
    n_seq,
    span_hidden,
    norm_gain,
    key_value_weight,
    prompt_key_value,
    span_offset,
    cont_query,
    continuation_key_value,
    cont_lengths,
):
    span_length, features = span_hidden.shape
    width = key_value_weight.shape[1]
    rows = span_length // n_seq
    cached = prompt_key_value.shape[0]
    tokens = cont_query.shape[1]
    n_x = n_set // 2
    halves = 2 if width % 512 == 0 else 1
    half = width // halves
    frequency = jnp.asarray(frequency_table())
    gain = norm_gain.reshape(features // HEAD_SIZE, HEAD_SIZE)
    dma = pltpu.SemaphoreType.DMA
    anywhere = pl.BlockSpec(memory_space=pl.ANY)
    span_rows, attended = pl.pallas_call(
        functools.partial(kernel, n_set, n_seq),
        out_shape=(
            jax.ShapeDtypeStruct((rows, width), BF16),
            jax.ShapeDtypeStruct((tokens, QUERY_HEADS * HEAD_SIZE), BF16),
        ),
        in_specs=[
            anywhere,
            anywhere,
            anywhere,
            anywhere,
            pl.BlockSpec(memory_space=pltpu.SMEM),
            anywhere,
            anywhere,
            anywhere,
        ],
        out_specs=(anywhere, pl.BlockSpec(memory_space=pltpu.VMEM)),
        scratch_shapes=[
            pltpu.VMEM((span_length, features), BF16),
            pltpu.VMEM((features // HEAD_SIZE, HEAD_SIZE), BF16),
            pltpu.VMEM((features, width), BF16),
            pltpu.VMEM((n_set, cached * n_seq, width), BF16),
            pltpu.VMEM((tokens, QUERY_HEADS * HEAD_SIZE), BF16),
            pltpu.VMEM((tokens, 2 * KEY_COLUMNS), BF16),
            pltpu.VMEM((8, HEAD_SIZE), F32),
            pltpu.VMEM((span_length, features), BF16),
            pltpu.VMEM((span_length, width), F32),
            pltpu.VMEM((halves, span_length, half), BF16),
            pltpu.VMEM((halves, n_seq, rows, half), BF16),
            pltpu.VMEM((8, span_length), F32),
            pltpu.VMEM((n_seq, 8, span_length), F32),
            pltpu.VMEM((span_length, HEAD_SIZE), F32),
            pltpu.VMEM((n_set, span_length, width), BF16),
            pltpu.VMEM((KEY_HEADS, GROUP * tokens, HEAD_SIZE), BF16),
            pltpu.VMEM((KEY_HEADS, GROUP * tokens, HEAD_SIZE), F32),
            pltpu.VMEM((KEY_HEADS, GROUP * tokens, 2 * HEAD_SIZE), F32),
            dma((n_set + halves + 5,)),
            dma,
            dma((n_seq,)),
            dma((n_seq,)),
            dma((halves, n_seq)),
            dma((halves, n_seq)),
            dma((n_seq,)),
            dma((n_seq,)),
            dma((n_seq, n_x)),
            dma((n_seq, n_x)),
            dma((n_seq, n_x)),
            dma((n_seq, n_x)),
            dma((n_seq,)),
            dma((n_seq,)),
            dma((n_seq, n_x)),
            dma((n_seq, n_x)),
            dma((n_seq, n_x)),
            dma((n_seq, n_x)),
        ],
        compiler_params=pltpu.CompilerParams(
            collective_id=0, has_side_effects=True, vmem_limit_bytes=48 * 1024 * 1024
        ),
        name="project_gather_attend",
    )(
        span_hidden,
        gain,
        key_value_weight,
        prompt_key_value,
        span_offset,
        cont_query,
        continuation_key_value,
        frequency,
    )
    live = jnp.arange(tokens, dtype=jnp.int32) < cont_lengths[0]
    return span_rows, jnp.where(live[:, None], attended, 0.0).astype(BF16)[None]


def solution(mesh):
    placed = (
        P("parts", "seq"),
        P("seq"),
        P("seq", "set"),
        P(("parts", "seq"), None),
        P("parts"),
        P(("parts", "set", "seq"), None, None),
        P(("parts", "set", "seq"), None, None),
        P(("parts", "set", "seq")),
    )
    return jax.shard_map(
        functools.partial(on_device, mesh.shape["set"], mesh.shape["seq"]),
        mesh=mesh,
        in_specs=placed,
        out_specs=(P(("parts", "seq"), "set"), P(("parts", "set", "seq"), None, None)),
        check_vma=False,
    )
```

```python
import functools
import math

import jax
import jax.numpy as jnp
import numpy as np
from jax import lax
from jax.experimental import pallas as pl
from jax.experimental.pallas import tpu as pltpu
from jax.sharding import PartitionSpec as P

MODEL_WIDTH = 8192
QUERY_HEADS = 64
KEY_HEADS = 8
HEAD_SIZE = 128
SPAN_LENGTH = 256
GROUP = QUERY_HEADS // KEY_HEADS
KEY_COLUMNS = KEY_HEADS * HEAD_SIZE

EPS = 1e-05
NEGATIVE_LARGE = -1e30
EXPONENT = HEAD_SIZE ** (-0.5) * math.log2(math.e)

MESH = pl.DeviceIdType.MESH
F32 = jnp.float32
BF16 = jnp.bfloat16


def frequency_table():
    index = np.arange(HEAD_SIZE // 2, dtype=np.float64)
    base = 500000.0 ** (-2.0 * index / HEAD_SIZE)
    wave = 2.0 * np.pi / base
    smooth = (8192.0 / wave - 1.0) / 3.0
    blended = (1.0 - smooth) * base / 8.0 + smooth * base
    table = np.where(wave < 2048.0, base, np.where(wave > 8192.0, base / 8.0, blended))
    row = np.concatenate([table, table]).astype(np.float32)
    return np.broadcast_to(row, (8, HEAD_SIZE)).copy()


def rotary_tables(frequency, start, rows):
    positions = (start + lax.broadcasted_iota(jnp.int32, (rows, HEAD_SIZE), 0)).astype(F32)
    angles = positions * frequency
    lane = lax.broadcasted_iota(jnp.int32, (rows, HEAD_SIZE), 1)
    sine = jnp.sin(angles)
    return jnp.cos(angles), jnp.where(lane < HEAD_SIZE // 2, -sine, sine)


def turn(value, cosine, sine):
    return value * cosine + pltpu.roll(value, HEAD_SIZE // 2, 1) * sine


def scores_of(query, keys):
    return lax.dot_general(query, keys, (((1,), (1,)), ((), ())), preferred_element_type=F32)


def with_ones(values):
    return jnp.concatenate([values, jnp.ones_like(values)], axis=1)


def kernel(
    n_set,
    n_seq,
    hidden_hbm,
    gain_hbm,
    weight_hbm,
    prompt_hbm,
    offset_smem,
    query_hbm,
    own_hbm,
    frequency_hbm,
    span_out,
    attended_out,
    hidden,
    gain,
    weight,
    prompt,
    query_in,
    own,
    frequency,
    scaled,
    partial,
    sending,
    received,
    square_mine,
    square_theirs,
    square_column,
    span,
    query,
    best,
    accum,
    outgoing,
    store_sem,
    load_sem,
    span_store_sem,
    square_send,
    square_recv,
    part_send,
    part_recv,
    pz_send,
    pz_recv,
    px_send,
    px_recv,
    pc_send,
    pc_recv,
    sz_send,
    sz_recv,
    sx_send,
    sx_recv,
    sc_send,
    sc_recv,
):
    n_x = n_set // 2
    me_set = lax.axis_index("set")
    me_seq = lax.axis_index("seq")
    me_x, me_core = me_set // 2, me_set % 2
    width = weight.shape[1]
    rows = span.shape[1] // n_seq
    cached = prompt.shape[1] // n_seq
    tokens = query_in.shape[0]
    halves = 2 if width % 512 == 0 else 1
    half = width // halves

    def seq_at(step):
        return (me_seq + step) % n_seq

    def set_at(step):
        return ((me_x + step) % n_x) * 2 + me_core

    twin = me_x * 2 + 1 - me_core

    def rows_of(which, count):
        return pl.ds(pl.multiple_of(which * count, count), count)

    loads = []

    def load(source, target):
        copy = pltpu.make_async_copy(source, target, load_sem.at[len(loads)])
        copy.start()
        loads.append(copy)
        return copy

    prompt_loads = [
        load(
            prompt_hbm.at[:, pl.ds(s * width, width)],
            prompt.at[s, rows_of(me_seq, cached), :],
        )
        for s in range(n_set)
    ]
    hidden_load = load(hidden_hbm, hidden)
    gain_load = load(gain_hbm, gain)
    weight_loads = [
        load(weight_hbm.at[:, pl.ds(i * half, half)], weight.at[:, pl.ds(i * half, half)])
        for i in range(halves)
    ]

    barrier = pltpu.get_barrier_semaphore()
    partners = [{"seq": seq_at(d)} for d in range(1, n_seq)]
    partners += [{"set": set_at(d)} for d in range(1, n_x)]
    partners += [{"set": twin}]
    for partner in partners:
        pl.semaphore_signal(barrier, inc=1, device_id=partner, device_id_type=MESH)
    for copy in prompt_loads:
        copy.wait()
    pl.semaphore_wait(barrier, len(partners))

    copies = []

    def remote(source, target, send_sem, recv_sem, device):
        return pltpu.make_async_remote_copy(
            src_ref=source,
            dst_ref=target,
            send_sem=send_sem,
            recv_sem=recv_sem,
            device_id=device,
            device_id_type=MESH,
        )

    def send(*args):
        copy = remote(*args)
        copy.start()
        copies.append(copy)
        return copy

    def other_seq(j):
        upper = (2 * me_seq) // n_seq
        low = j + (j - me_seq + n_seq) // n_seq
        down = n_seq - 1 - j
        high = down - (me_seq - down + n_seq) // n_seq
        return low + upper * (high - low)

    others = range(n_seq - 1)

    def prompt_block(s, z):
        return prompt.at[s, rows_of(z, cached), :]

    def span_block(s, i, z):
        return span.at[s * halves + i, rows_of(z, rows), :]

    for j in reversed(others):
        block, z = prompt_block(me_set, me_seq), other_seq(j)
        send(block, block, pz_send.at[z], pz_recv.at[me_seq], {"seq": z})

    hidden_load.wait()
    gain_load.wait()
    squares = jnp.zeros((hidden.shape[0], HEAD_SIZE), F32)
    for i in range(hidden.shape[1] // HEAD_SIZE):
        block = hidden[:, i * HEAD_SIZE : (i + 1) * HEAD_SIZE].astype(F32)
        squares += block * block
        scaled[:, i * HEAD_SIZE : (i + 1) * HEAD_SIZE] = (
            block * gain[i : i + 1, :].astype(F32)
        ).astype(BF16)
    square_row = jnp.sum(squares.T, axis=0, keepdims=True)
    square_mine[...] = jnp.broadcast_to(square_row, square_mine.shape)

    for i in range(halves):
        weight_loads[i].wait()
        if i == 0:
            for j in reversed(others):
                z = other_seq(j)
                send(
                    square_mine,
                    square_theirs.at[me_seq],
                    square_send.at[z],
                    square_recv.at[me_seq],
                    {"seq": z},
                )
        columns = pl.ds(i * half, half)
        product = jnp.dot(scaled[...], weight[:, columns], preferred_element_type=F32)
        partial[:, columns] = product
        sending[i] = product.astype(BF16)
        for j in reversed(others):
            z = other_seq(j)
            send(
                sending.at[i, rows_of(z, rows), :],
                received.at[i, me_seq],
                part_send.at[i, z],
                part_recv.at[i, me_seq],
                {"seq": z},
            )

    own_load = load(own_hbm.at[0], own)
    query_load = load(query_hbm.at[0], query_in)
    frequency_load = load(frequency_hbm, frequency)

    def pass_prompt(j):
        z = other_seq(j)
        block = prompt_block(me_set, z)
        remote(block, block, pz_send.at[z], pz_recv.at[z], {"seq": z}).wait_recv()
        for e in range(1, n_x):
            send(block, block, px_send.at[z, e], px_recv.at[z, e], {"set": set_at(e)})
        send(block, block, pc_send.at[z, 0], pc_recv.at[z, 0], {"set": twin})

    def pass_prompt_twin(j):
        z = other_seq(j)
        for e in range(1, n_x):
            come = prompt_block(set_at(n_x - e), z)
            remote(come, come, px_send.at[z, e], px_recv.at[z, e], {"set": twin}).wait_recv()
            send(come, come, pc_send.at[z, e], pc_recv.at[z, e], {"set": twin})

    frequency_load.wait()
    offset = offset_smem[0]
    cosine, sine = rotary_tables(frequency[0:1, :], offset + SPAN_LENGTH, tokens)
    span_cosine, span_sine = rotary_tables(frequency[0:1, :], offset + me_seq * rows, rows)
    own_load.wait()
    query_load.wait()

    causal = jnp.concatenate(
        [
            lax.broadcasted_iota(jnp.int32, (tokens, tokens), 0)
            >= lax.broadcasted_iota(jnp.int32, (tokens, tokens), 1)
        ]
        * GROUP,
        axis=0,
    )

    def columns_of(head):
        return pl.ds(pl.multiple_of(head * HEAD_SIZE, HEAD_SIZE), HEAD_SIZE)

    def attend_own(head, carry):
        for g in range(GROUP):
            raw = query_in[:, columns_of(head * GROUP + g)].astype(F32)
            query[head, pl.ds(g * tokens, tokens), :] = turn(raw, cosine, sine).astype(BF16)
        keys = turn(own[:, columns_of(head)].astype(F32), cosine, sine).astype(BF16)
        values = own[:, columns_of(head + KEY_HEADS)]
        scores = jnp.where(causal, scores_of(query[head], keys), NEGATIVE_LARGE)
        top = jnp.max(scores, axis=1, keepdims=True)
        weights = jnp.exp2((scores - top) * EXPONENT).astype(BF16)
        best[head] = jnp.broadcast_to(top, best.shape[1:])
        accum[head] = jnp.dot(weights, with_ones(values), preferred_element_type=F32)
        return carry

    lax.fori_loop(0, KEY_HEADS // 4, attend_own, 0)
    for j in others:
        pass_prompt(j)
    lax.fori_loop(KEY_HEADS // 4, KEY_HEADS, attend_own, 0)
    for j in others:
        pass_prompt_twin(j)

    square_total = square_mine[...]
    for j in others:
        z = other_seq(j)
        remote(
            square_mine, square_theirs.at[z], square_send.at[z], square_recv.at[z], {"seq": z}
        ).wait_recv()
        square_total += square_theirs[z]
    square_column[...] = jnp.broadcast_to(
        square_total[0:1, :], (HEAD_SIZE, square_total.shape[1])
    ).T
    inverse = lax.rsqrt(square_column[rows_of(me_seq, rows), :] / MODEL_WIDTH + EPS)

    def finish(i):
        for j in others:
            z = other_seq(j)
            remote(
                sending.at[i, rows_of(z, rows), :],
                received.at[i, z],
                part_send.at[i, z],
                part_recv.at[i, z],
                {"seq": z},
            ).wait_recv()
        for c in range(half // HEAD_SIZE):
            column = i * half + c * HEAD_SIZE
            block = partial[rows_of(me_seq, rows), pl.ds(column, HEAD_SIZE)]
            for j in others:
                block += received[i, other_seq(j), :, pl.ds(c * HEAD_SIZE, HEAD_SIZE)].astype(F32)
            block = block * inverse
            turned = turn(block, span_cosine, span_sine)
            is_key = me_set * width + column < KEY_COLUMNS
            span[
                me_set * halves + i, rows_of(me_seq, rows), pl.ds(c * HEAD_SIZE, HEAD_SIZE)
            ] = jnp.where(is_key, turned, block).astype(BF16)
        mine = span_block(me_set, i, me_seq)
        for e in range(1, n_x):
            send(
                mine, mine, sx_send.at[i, me_seq, e], sx_recv.at[i, me_seq, e], {"set": set_at(e)}
            )
        for j in others:
            z = other_seq(j)
            send(mine, mine, sz_send.at[i, z], sz_recv.at[i, me_seq], {"seq": z})
        send(mine, mine, sc_send.at[i, me_seq, 0], sc_recv.at[i, me_seq, 0], {"set": twin})
        span_store(i).start()

    def span_store(i):
        return pltpu.make_async_copy(
            span_block(me_set, i, me_seq),
            span_out.at[:, pl.ds(i * half, half)],
            span_store_sem.at[i],
        )

    def pass_span(i, j):
        z = other_seq(j)
        block = span_block(me_set, i, z)
        remote(block, block, sz_send.at[i, z], sz_recv.at[i, z], {"seq": z}).wait_recv()
        for e in range(1, n_x):
            send(block, block, sx_send.at[i, z, e], sx_recv.at[i, z, e], {"set": set_at(e)})
        send(block, block, sc_send.at[i, z, 0], sc_recv.at[i, z, 0], {"set": twin})

    def pass_span_twin(i, z):
        for e in range(1, n_x):
            come = span_block(set_at(n_x - e), i, z)
            remote(
                come, come, sx_send.at[i, z, e], sx_recv.at[i, z, e], {"set": twin}
            ).wait_recv()
            send(come, come, sc_send.at[i, z, e], sc_recv.at[i, z, e], {"set": twin})

    def span_arrived(i):
        twin_x = twin
        for z in range(n_seq):
            for e in range(n_x):
                come = span_block(twin_x, i, z)
                remote(
                    come, come, sc_send.at[i, z, e], sc_recv.at[i, z, e], {"set": twin}
                ).wait_recv()

    def attend_more(head, keys, values, mask):
        scores = scores_of(query[head], keys)
        if mask is not None:
            scores = jnp.where(mask, scores, NEGATIVE_LARGE)
        old = best[head]
        top = jnp.maximum(old, jnp.max(scores, axis=1, keepdims=True))
        spread = jnp.concatenate([top] * (scores.shape[1] // HEAD_SIZE), axis=1)
        weights = jnp.exp2((scores - spread) * EXPONENT).astype(BF16)
        shrink = jnp.exp2((old - top) * EXPONENT)
        total = accum[head] * jnp.concatenate([shrink, shrink], axis=1) + jnp.dot(
            weights, with_ones(values), preferred_element_type=F32
        )
        return top, total

    per_set = width // HEAD_SIZE
    per_part = half // HEAD_SIZE
    live = lax.broadcasted_iota(jnp.int32, (1, prompt.shape[1]), 1) < offset

    def prompt_head(head):
        return prompt[head // per_set, :, columns_of(head % per_set)]

    def span_head(head):
        start = head % per_part * HEAD_SIZE
        return span[head // per_part, :, start : start + HEAD_SIZE]

    def attend_prompt(head, carry):
        top, total = attend_more(head, prompt_head(head), prompt_head(head + KEY_HEADS), live)
        best[head] = top
        accum[head] = total
        return carry

    def store_of(head):
        columns = pl.ds(head * GROUP * HEAD_SIZE, GROUP * HEAD_SIZE)
        return pltpu.make_async_copy(
            outgoing.at[:, columns], attended_out.at[:, columns], store_sem.at[head]
        )

    def attend_span(head):
        top, total = attend_more(head, span_head(head), span_head(head + KEY_HEADS), None)
        mixed = (total[:, :HEAD_SIZE] / total[:, HEAD_SIZE:]).astype(BF16)
        for g in range(GROUP):
            column = (head * GROUP + g) * HEAD_SIZE
            outgoing[:, column : column + HEAD_SIZE] = mixed[g * tokens : (g + 1) * tokens, :]
        store_of(head).start()

    def prompt_arrived():
        for j in others:
            z = other_seq(j)
            for e in range(n_x):
                come = prompt_block(twin, z)
                remote(
                    come, come, pc_send.at[z, e], pc_recv.at[z, e], {"set": twin}
                ).wait_recv()

    finish(0)
    prompt_arrived()
    middle = KEY_HEADS // 2
    lax.fori_loop(0, middle, attend_prompt, 0)
    for i in range(1, halves):
        finish(i)
    pass_span_twin(0, me_seq)
    for j in others:
        pass_span(0, j)
        cut = [middle + (KEY_HEADS - middle) * k // (n_seq - 1) for k in (j, j + 1)]
        if cut[0] < cut[1]:
            lax.fori_loop(cut[0], cut[1], attend_prompt, 0)
    for j in others:
        pass_span_twin(0, other_seq(j))
    for i in range(halves):
        heads = [h for h in range(KEY_HEADS) if h % per_set // per_part == i]
        steps = []
        if i + 1 < halves:
            steps = [functools.partial(pass_span_twin, i + 1, me_seq)]
            steps += [functools.partial(pass_span, i + 1, j) for j in others]
        for step in steps[:3]:
            step()
        span_arrived(i)
        for step in steps[3:]:
            step()
        for head in heads:
            attend_span(head)
        if i + 1 < halves:
            for j in others:
                pass_span_twin(i + 1, other_seq(j))

    for copy in copies:
        copy.wait_send()
    for i in range(halves):
        span_store(i).wait()
    for head in range(KEY_HEADS):
        store_of(head).wait()


def on_device(
    n_set,
    n_seq,
    span_hidden,
    norm_gain,
    key_value_weight,
    prompt_key_value,
    span_offset,
    cont_query,
    continuation_key_value,
    cont_lengths,
):
    span_length, features = span_hidden.shape
    width = key_value_weight.shape[1]
    rows = span_length // n_seq
    cached = prompt_key_value.shape[0]
    tokens = cont_query.shape[1]
    n_x = n_set // 2
    halves = 2 if width % 512 == 0 else 1
    half = width // halves
    frequency = jnp.asarray(frequency_table())
    gain = norm_gain.reshape(features // HEAD_SIZE, HEAD_SIZE)
    dma = pltpu.SemaphoreType.DMA
    anywhere = pl.BlockSpec(memory_space=pl.ANY)
    span_rows, attended = pl.pallas_call(
        functools.partial(kernel, n_set, n_seq),
        out_shape=(
            jax.ShapeDtypeStruct((rows, width), BF16),
            jax.ShapeDtypeStruct((tokens, QUERY_HEADS * HEAD_SIZE), BF16),
        ),
        in_specs=[
            anywhere,
            anywhere,
            anywhere,
            anywhere,
            pl.BlockSpec(memory_space=pltpu.SMEM),
            anywhere,
            anywhere,
            anywhere,
        ],
        out_specs=(anywhere, anywhere),
        scratch_shapes=[
            pltpu.VMEM((span_length, features), BF16),
            pltpu.VMEM((features // HEAD_SIZE, HEAD_SIZE), BF16),
            pltpu.VMEM((features, width), BF16),
            pltpu.VMEM((n_set, cached * n_seq, width), BF16),
            pltpu.VMEM((tokens, QUERY_HEADS * HEAD_SIZE), BF16),
            pltpu.VMEM((tokens, 2 * KEY_COLUMNS), BF16),
            pltpu.VMEM((8, HEAD_SIZE), F32),
            pltpu.VMEM((span_length, features), BF16),
            pltpu.VMEM((span_length, width), F32),
            pltpu.VMEM((halves, span_length, half), BF16),
            pltpu.VMEM((halves, n_seq, rows, half), BF16),
            pltpu.VMEM((8, span_length), F32),
            pltpu.VMEM((n_seq, 8, span_length), F32),
            pltpu.VMEM((span_length, HEAD_SIZE), F32),
            pltpu.VMEM((n_set * halves, span_length, half), BF16),
            pltpu.VMEM((KEY_HEADS, GROUP * tokens, HEAD_SIZE), BF16),
            pltpu.VMEM((KEY_HEADS, GROUP * tokens, HEAD_SIZE), F32),
            pltpu.VMEM((KEY_HEADS, GROUP * tokens, 2 * HEAD_SIZE), F32),
            pltpu.VMEM((tokens, QUERY_HEADS * HEAD_SIZE), BF16),
            dma((KEY_HEADS,)),
            dma((n_set + halves + 5,)),
            dma((halves,)),
            dma((n_seq,)),
            dma((n_seq,)),
            dma((halves, n_seq)),
            dma((halves, n_seq)),
            dma((n_seq,)),
            dma((n_seq,)),
            dma((n_seq, n_x)),
            dma((n_seq, n_x)),
            dma((n_seq, n_x)),
            dma((n_seq, n_x)),
            dma((halves, n_seq)),
            dma((halves, n_seq)),
            dma((halves, n_seq, n_x)),
            dma((halves, n_seq, n_x)),
            dma((halves, n_seq, n_x)),
            dma((halves, n_seq, n_x)),
        ],
        compiler_params=pltpu.CompilerParams(
            collective_id=0, has_side_effects=True, vmem_limit_bytes=67043328
        ),
        name="project_gather_attend",
    )(
        span_hidden,
        gain,
        key_value_weight,
        prompt_key_value,
        span_offset,
        cont_query,
        continuation_key_value,
        frequency,
    )
    live = jnp.arange(tokens, dtype=jnp.int32) < cont_lengths[0]
    return span_rows, jnp.where(live[:, None], attended, 0.0).astype(BF16)[None]


def solution(mesh):
    placed = (
        P("parts", "seq"),
        P("seq"),
        P("seq", "set"),
        P(("parts", "seq"), None),
        P("parts"),
        P(("parts", "set", "seq"), None, None),
        P(("parts", "set", "seq"), None, None),
        P(("parts", "set", "seq")),
    )
    return jax.shard_map(
        functools.partial(on_device, mesh.shape["set"], mesh.shape["seq"]),
        mesh=mesh,
        in_specs=placed,
        out_specs=(P(("parts", "seq"), "set"), P(("parts", "set", "seq"), None, None)),
        check_vma=False,
    )
```

```python
import functools
import math

import jax
import jax.numpy as jnp
import numpy as np
from jax import lax
from jax.experimental import pallas as pl
from jax.experimental.pallas import tpu as pltpu
from jax.sharding import PartitionSpec as P

MODEL_WIDTH = 8192
QUERY_HEADS = 64
KEY_HEADS = 8
HEAD_SIZE = 128
SPAN_LENGTH = 256
GROUP = QUERY_HEADS // KEY_HEADS
KEY_COLUMNS = KEY_HEADS * HEAD_SIZE

EPS = 1e-05
NEGATIVE_LARGE = -1e30
EXPONENT = HEAD_SIZE ** (-0.5) * math.log2(math.e)

MESH = pl.DeviceIdType.MESH
F32 = jnp.float32
BF16 = jnp.bfloat16


def frequency_table():
    index = np.arange(HEAD_SIZE // 2, dtype=np.float64)
    base = 500000.0 ** (-2.0 * index / HEAD_SIZE)
    wave = 2.0 * np.pi / base
    smooth = (8192.0 / wave - 1.0) / 3.0
    blended = (1.0 - smooth) * base / 8.0 + smooth * base
    table = np.where(wave < 2048.0, base, np.where(wave > 8192.0, base / 8.0, blended))
    row = np.concatenate([table, table]).astype(np.float32)
    return np.broadcast_to(row, (8, HEAD_SIZE)).copy()


def rotary_tables(frequency, start, rows):
    positions = (start + lax.broadcasted_iota(jnp.int32, (rows, HEAD_SIZE), 0)).astype(F32)
    angles = positions * frequency
    lane = lax.broadcasted_iota(jnp.int32, (rows, HEAD_SIZE), 1)
    sine = jnp.sin(angles)
    return jnp.cos(angles), jnp.where(lane < HEAD_SIZE // 2, -sine, sine)


def turn(value, cosine, sine):
    return value * cosine + pltpu.roll(value, HEAD_SIZE // 2, 1) * sine


def scores_of(query, keys):
    return lax.dot_general(query, keys, (((1,), (1,)), ((), ())), preferred_element_type=F32)


def with_ones(values):
    return jnp.concatenate([values, jnp.ones_like(values)], axis=1)


def kernel(
    n_set,
    n_seq,
    hidden_hbm,
    gain_hbm,
    weight_hbm,
    prompt_hbm,
    offset_smem,
    length_smem,
    query_hbm,
    own_hbm,
    frequency_hbm,
    span_out,
    attended_out,
    hidden,
    gain,
    weight,
    prompt,
    query_in,
    own,
    frequency,
    scaled,
    partial,
    sending,
    received,
    square_mine,
    square_theirs,
    square_column,
    span,
    query,
    best,
    accum,
    outgoing,
    store_sem,
    load_sem,
    span_store_sem,
    square_send,
    square_recv,
    part_send,
    part_recv,
    pz_send,
    pz_recv,
    px_send,
    px_recv,
    pc_send,
    pc_recv,
    sz_send,
    sz_recv,
    sx_send,
    sx_recv,
    sc_send,
    sc_recv,
):
    n_x = n_set // 2
    me_set = lax.axis_index("set")
    me_seq = lax.axis_index("seq")
    me_x, me_core = me_set // 2, me_set % 2
    width = weight.shape[1]
    rows = span.shape[1] // n_seq
    cached = prompt.shape[1] // n_seq
    tokens = query_in.shape[0]
    halves = 2 if width % 512 == 0 else 1
    half = width // halves

    def seq_at(step):
        return (me_seq + step) % n_seq

    def set_at(step):
        return ((me_x + step) % n_x) * 2 + me_core

    twin = me_x * 2 + 1 - me_core

    def rows_of(which, count):
        return pl.ds(pl.multiple_of(which * count, count), count)

    loads = []

    def load(source, target):
        copy = pltpu.make_async_copy(source, target, load_sem.at[len(loads)])
        copy.start()
        loads.append(copy)
        return copy

    prompt_loads = [
        load(
            prompt_hbm.at[:, pl.ds(s * width, width)],
            prompt.at[s, rows_of(me_seq, cached), :],
        )
        for s in range(n_set)
    ]
    hidden_load = load(hidden_hbm, hidden)
    gain_load = load(gain_hbm, gain)
    weight_loads = [
        load(weight_hbm.at[:, pl.ds(i * half, half)], weight.at[:, pl.ds(i * half, half)])
        for i in range(halves)
    ]

    barrier = pltpu.get_barrier_semaphore()
    partners = [{"seq": seq_at(d)} for d in range(1, n_seq)]
    partners += [{"set": set_at(d)} for d in range(1, n_x)]
    partners += [{"set": twin}]
    for partner in partners:
        pl.semaphore_signal(barrier, inc=1, device_id=partner, device_id_type=MESH)
    for copy in prompt_loads:
        copy.wait()
    pl.semaphore_wait(barrier, len(partners))

    copies = []

    def remote(source, target, send_sem, recv_sem, device):
        return pltpu.make_async_remote_copy(
            src_ref=source,
            dst_ref=target,
            send_sem=send_sem,
            recv_sem=recv_sem,
            device_id=device,
            device_id_type=MESH,
        )

    def send(*args):
        copy = remote(*args)
        copy.start()
        copies.append(copy)
        return copy

    def other_seq(j):
        upper = (2 * me_seq) // n_seq
        low = j + (j - me_seq + n_seq) // n_seq
        down = n_seq - 1 - j
        high = down - (me_seq - down + n_seq) // n_seq
        return low + upper * (high - low)

    others = range(n_seq - 1)

    def prompt_block(s, z):
        return prompt.at[s, rows_of(z, cached), :]

    def span_block(s, i, z):
        return span.at[s * halves + i, rows_of(z, rows), :]

    for j in reversed(others):
        block, z = prompt_block(me_set, me_seq), other_seq(j)
        send(block, block, pz_send.at[z], pz_recv.at[me_seq], {"seq": z})

    hidden_load.wait()
    gain_load.wait()
    squares = jnp.zeros((hidden.shape[0], HEAD_SIZE), F32)
    for i in range(hidden.shape[1] // HEAD_SIZE):
        block = hidden[:, i * HEAD_SIZE : (i + 1) * HEAD_SIZE].astype(F32)
        squares += block * block
        scaled[:, i * HEAD_SIZE : (i + 1) * HEAD_SIZE] = (
            block * gain[i : i + 1, :].astype(F32)
        ).astype(BF16)
    square_row = jnp.sum(squares.T, axis=0, keepdims=True)
    square_mine[...] = jnp.broadcast_to(square_row, square_mine.shape)

    for i in range(halves):
        weight_loads[i].wait()
        if i == 0:
            for j in reversed(others):
                z = other_seq(j)
                send(
                    square_mine,
                    square_theirs.at[me_seq],
                    square_send.at[z],
                    square_recv.at[me_seq],
                    {"seq": z},
                )
        columns = pl.ds(i * half, half)
        product = jnp.dot(scaled[...], weight[:, columns], preferred_element_type=F32)
        partial[:, columns] = product
        sending[i] = product.astype(BF16)
        for j in reversed(others):
            z = other_seq(j)
            send(
                sending.at[i, rows_of(z, rows), :],
                received.at[i, me_seq],
                part_send.at[i, z],
                part_recv.at[i, me_seq],
                {"seq": z},
            )

    own_load = load(own_hbm.at[0], own)
    query_load = load(query_hbm.at[0], query_in)
    frequency_load = load(frequency_hbm, frequency)

    def pass_prompt(j):
        z = other_seq(j)
        block = prompt_block(me_set, z)
        remote(block, block, pz_send.at[z], pz_recv.at[z], {"seq": z}).wait_recv()
        for e in range(1, n_x):
            send(block, block, px_send.at[z, e], px_recv.at[z, e], {"set": set_at(e)})
        send(block, block, pc_send.at[z, 0], pc_recv.at[z, 0], {"set": twin})

    def pass_prompt_twin(j):
        z = other_seq(j)
        for e in range(1, n_x):
            come = prompt_block(set_at(n_x - e), z)
            remote(come, come, px_send.at[z, e], px_recv.at[z, e], {"set": twin}).wait_recv()
            send(come, come, pc_send.at[z, e], pc_recv.at[z, e], {"set": twin})

    frequency_load.wait()
    offset = offset_smem[0]
    cosine, sine = rotary_tables(frequency[0:1, :], offset + SPAN_LENGTH, tokens)
    span_cosine, span_sine = rotary_tables(frequency[0:1, :], offset + me_seq * rows, rows)
    own_load.wait()
    query_load.wait()

    causal = jnp.concatenate(
        [
            lax.broadcasted_iota(jnp.int32, (tokens, tokens), 0)
            >= lax.broadcasted_iota(jnp.int32, (tokens, tokens), 1)
        ]
        * GROUP,
        axis=0,
    )

    def columns_of(head):
        return pl.ds(pl.multiple_of(head * HEAD_SIZE, HEAD_SIZE), HEAD_SIZE)

    def attend_own(head, carry):
        for g in range(GROUP):
            raw = query_in[:, columns_of(head * GROUP + g)].astype(F32)
            query[head, pl.ds(g * tokens, tokens), :] = turn(raw, cosine, sine).astype(BF16)
        keys = turn(own[:, columns_of(head)].astype(F32), cosine, sine).astype(BF16)
        values = own[:, columns_of(head + KEY_HEADS)]
        scores = jnp.where(causal, scores_of(query[head], keys), NEGATIVE_LARGE)
        top = jnp.max(scores, axis=1, keepdims=True)
        weights = jnp.exp2((scores - top) * EXPONENT).astype(BF16)
        best[head] = jnp.broadcast_to(top, best.shape[1:])
        accum[head] = jnp.dot(weights, with_ones(values), preferred_element_type=F32)
        return carry

    lax.fori_loop(0, KEY_HEADS // 4, attend_own, 0)
    for j in others:
        pass_prompt(j)
    lax.fori_loop(KEY_HEADS // 4, KEY_HEADS, attend_own, 0)
    for j in others:
        pass_prompt_twin(j)

    square_total = square_mine[...]
    for j in others:
        z = other_seq(j)
        remote(
            square_mine, square_theirs.at[z], square_send.at[z], square_recv.at[z], {"seq": z}
        ).wait_recv()
        square_total += square_theirs[z]
    square_column[...] = jnp.broadcast_to(
        square_total[0:1, :], (HEAD_SIZE, square_total.shape[1])
    ).T
    inverse = lax.rsqrt(square_column[rows_of(me_seq, rows), :] / MODEL_WIDTH + EPS)

    def finish(i):
        for j in others:
            z = other_seq(j)
            remote(
                sending.at[i, rows_of(z, rows), :],
                received.at[i, z],
                part_send.at[i, z],
                part_recv.at[i, z],
                {"seq": z},
            ).wait_recv()
        for c in range(half // HEAD_SIZE):
            column = i * half + c * HEAD_SIZE
            block = partial[rows_of(me_seq, rows), pl.ds(column, HEAD_SIZE)]
            for j in others:
                block += received[i, other_seq(j), :, pl.ds(c * HEAD_SIZE, HEAD_SIZE)].astype(F32)
            block = block * inverse
            turned = turn(block, span_cosine, span_sine)
            is_key = me_set * width + column < KEY_COLUMNS
            span[
                me_set * halves + i, rows_of(me_seq, rows), pl.ds(c * HEAD_SIZE, HEAD_SIZE)
            ] = jnp.where(is_key, turned, block).astype(BF16)
        mine = span_block(me_set, i, me_seq)
        for e in range(1, n_x):
            send(
                mine, mine, sx_send.at[i, me_seq, e], sx_recv.at[i, me_seq, e], {"set": set_at(e)}
            )
        for j in others:
            z = other_seq(j)
            send(mine, mine, sz_send.at[i, z], sz_recv.at[i, me_seq], {"seq": z})
        send(mine, mine, sc_send.at[i, me_seq, 0], sc_recv.at[i, me_seq, 0], {"set": twin})
        span_store(i).start()

    def span_store(i):
        return pltpu.make_async_copy(
            span_block(me_set, i, me_seq),
            span_out.at[:, pl.ds(i * half, half)],
            span_store_sem.at[i],
        )

    def pass_span(i, j):
        z = other_seq(j)
        block = span_block(me_set, i, z)
        remote(block, block, sz_send.at[i, z], sz_recv.at[i, z], {"seq": z}).wait_recv()
        for e in range(1, n_x):
            send(block, block, sx_send.at[i, z, e], sx_recv.at[i, z, e], {"set": set_at(e)})
        send(block, block, sc_send.at[i, z, 0], sc_recv.at[i, z, 0], {"set": twin})

    def pass_span_twin(i, z):
        for e in range(1, n_x):
            come = span_block(set_at(n_x - e), i, z)
            remote(
                come, come, sx_send.at[i, z, e], sx_recv.at[i, z, e], {"set": twin}
            ).wait_recv()
            send(come, come, sc_send.at[i, z, e], sc_recv.at[i, z, e], {"set": twin})

    def span_arrived(i):
        twin_x = twin
        for z in range(n_seq):
            for e in range(n_x):
                come = span_block(twin_x, i, z)
                remote(
                    come, come, sc_send.at[i, z, e], sc_recv.at[i, z, e], {"set": twin}
                ).wait_recv()

    def attend_more(head, keys, values, mask):
        scores = scores_of(query[head], keys)
        if mask is not None:
            scores = jnp.where(mask, scores, NEGATIVE_LARGE)
        old = best[head]
        top = jnp.maximum(old, jnp.max(scores, axis=1, keepdims=True))
        spread = jnp.concatenate([top] * (scores.shape[1] // HEAD_SIZE), axis=1)
        weights = jnp.exp2((scores - spread) * EXPONENT).astype(BF16)
        shrink = jnp.exp2((old - top) * EXPONENT)
        total = accum[head] * jnp.concatenate([shrink, shrink], axis=1) + jnp.dot(
            weights, with_ones(values), preferred_element_type=F32
        )
        return top, total

    kept = lax.broadcasted_iota(jnp.int32, (tokens, HEAD_SIZE), 0) < length_smem[0]
    per_set = width // HEAD_SIZE
    per_part = half // HEAD_SIZE
    live = lax.broadcasted_iota(jnp.int32, (1, prompt.shape[1]), 1) < offset

    def prompt_head(head):
        return prompt[head // per_set, :, columns_of(head % per_set)]

    def span_head(head):
        start = head % per_part * HEAD_SIZE
        return span[head // per_part, :, start : start + HEAD_SIZE]

    def attend_prompt(head, carry):
        top, total = attend_more(head, prompt_head(head), prompt_head(head + KEY_HEADS), live)
        best[head] = top
        accum[head] = total
        return carry

    def store_of(head):
        columns = pl.ds(head * GROUP * HEAD_SIZE, GROUP * HEAD_SIZE)
        return pltpu.make_async_copy(
            outgoing.at[:, columns], attended_out.at[:, columns], store_sem.at[head]
        )

    def attend_span(head):
        top, total = attend_more(head, span_head(head), span_head(head + KEY_HEADS), None)
        mixed = total[:, :HEAD_SIZE] / total[:, HEAD_SIZE:]
        for g in range(GROUP):
            column = (head * GROUP + g) * HEAD_SIZE
            outgoing[:, column : column + HEAD_SIZE] = jnp.where(
                kept, mixed[g * tokens : (g + 1) * tokens, :], 0.0
            ).astype(BF16)
        store_of(head).start()

    def prompt_arrived():
        for j in others:
            z = other_seq(j)
            for e in range(n_x):
                come = prompt_block(twin, z)
                remote(
                    come, come, pc_send.at[z, e], pc_recv.at[z, e], {"set": twin}
                ).wait_recv()

    finish(0)
    prompt_arrived()
    middle = KEY_HEADS // 2
    lax.fori_loop(0, middle, attend_prompt, 0)
    for i in range(1, halves):
        finish(i)
    pass_span_twin(0, me_seq)
    for j in others:
        pass_span(0, j)
        cut = [middle + (KEY_HEADS - middle) * k // (n_seq - 1) for k in (j, j + 1)]
        if cut[0] < cut[1]:
            lax.fori_loop(cut[0], cut[1], attend_prompt, 0)
    for j in others:
        pass_span_twin(0, other_seq(j))
    for i in range(halves):
        heads = [h for h in range(KEY_HEADS) if h % per_set // per_part == i]
        steps = []
        if i + 1 < halves:
            steps = [functools.partial(pass_span_twin, i + 1, me_seq)]
            steps += [functools.partial(pass_span, i + 1, j) for j in others]
        for step in steps[:3]:
            step()
        span_arrived(i)
        for step in steps[3:]:
            step()
        for head in heads:
            attend_span(head)
        if i + 1 < halves:
            for j in others:
                pass_span_twin(i + 1, other_seq(j))

    for copy in copies:
        copy.wait_send()
    for i in range(halves):
        span_store(i).wait()
    for head in range(KEY_HEADS):
        store_of(head).wait()


def hand_on(chunks, span_in, attended_in, span_out, attended_out, rows, tokens, in_sem, out_sem):
    step = tokens.shape[0] // chunks
    parts = [pl.ds(c * step, step) for c in range(chunks)]
    ins = [
        pltpu.make_async_copy(attended_in.at[part, :], tokens.at[part, :], in_sem.at[c])
        for c, part in enumerate(parts)
    ] + [pltpu.make_async_copy(span_in, rows, in_sem.at[chunks])]
    outs = [
        pltpu.make_async_copy(tokens.at[part, :], attended_out.at[0, part, :], out_sem.at[c])
        for c, part in enumerate(parts)
    ] + [pltpu.make_async_copy(rows, span_out, out_sem.at[chunks])]
    for copy in ins:
        copy.start()
    for arriving, leaving in zip(ins, outs):
        arriving.wait()
        leaving.start()
    for copy in outs:
        copy.wait()


def on_device(
    n_set,
    n_seq,
    span_hidden,
    norm_gain,
    key_value_weight,
    prompt_key_value,
    span_offset,
    cont_query,
    continuation_key_value,
    cont_lengths,
):
    span_length, features = span_hidden.shape
    width = key_value_weight.shape[1]
    rows = span_length // n_seq
    cached = prompt_key_value.shape[0]
    tokens = cont_query.shape[1]
    n_x = n_set // 2
    halves = 2 if width % 512 == 0 else 1
    half = width // halves
    frequency = jnp.asarray(frequency_table())
    gain = norm_gain.reshape(features // HEAD_SIZE, HEAD_SIZE)
    dma = pltpu.SemaphoreType.DMA
    anywhere = pl.BlockSpec(memory_space=pl.ANY)
    span_rows, attended = pl.pallas_call(
        functools.partial(kernel, n_set, n_seq),
        out_shape=(
            jax.ShapeDtypeStruct((rows, width), BF16),
            jax.ShapeDtypeStruct((tokens, QUERY_HEADS * HEAD_SIZE), BF16),
        ),
        in_specs=[
            anywhere,
            anywhere,
            anywhere,
            anywhere,
            pl.BlockSpec(memory_space=pltpu.SMEM),
            pl.BlockSpec(memory_space=pltpu.SMEM),
            anywhere,
            anywhere,
            anywhere,
        ],
        out_specs=(anywhere, anywhere),
        scratch_shapes=[
            pltpu.VMEM((span_length, features), BF16),
            pltpu.VMEM((features // HEAD_SIZE, HEAD_SIZE), BF16),
            pltpu.VMEM((features, width), BF16),
            pltpu.VMEM((n_set, cached * n_seq, width), BF16),
            pltpu.VMEM((tokens, QUERY_HEADS * HEAD_SIZE), BF16),
            pltpu.VMEM((tokens, 2 * KEY_COLUMNS), BF16),
            pltpu.VMEM((8, HEAD_SIZE), F32),
            pltpu.VMEM((span_length, features), BF16),
            pltpu.VMEM((span_length, width), F32),
            pltpu.VMEM((halves, span_length, half), BF16),
            pltpu.VMEM((halves, n_seq, rows, half), BF16),
            pltpu.VMEM((8, span_length), F32),
            pltpu.VMEM((n_seq, 8, span_length), F32),
            pltpu.VMEM((span_length, HEAD_SIZE), F32),
            pltpu.VMEM((n_set * halves, span_length, half), BF16),
            pltpu.VMEM((KEY_HEADS, GROUP * tokens, HEAD_SIZE), BF16),
            pltpu.VMEM((KEY_HEADS, GROUP * tokens, HEAD_SIZE), F32),
            pltpu.VMEM((KEY_HEADS, GROUP * tokens, 2 * HEAD_SIZE), F32),
            pltpu.VMEM((tokens, QUERY_HEADS * HEAD_SIZE), BF16),
            dma((KEY_HEADS,)),
            dma((n_set + halves + 5,)),
            dma((halves,)),
            dma((n_seq,)),
            dma((n_seq,)),
            dma((halves, n_seq)),
            dma((halves, n_seq)),
            dma((n_seq,)),
            dma((n_seq,)),
            dma((n_seq, n_x)),
            dma((n_seq, n_x)),
            dma((n_seq, n_x)),
            dma((n_seq, n_x)),
            dma((halves, n_seq)),
            dma((halves, n_seq)),
            dma((halves, n_seq, n_x)),
            dma((halves, n_seq, n_x)),
            dma((halves, n_seq, n_x)),
            dma((halves, n_seq, n_x)),
        ],
        compiler_params=pltpu.CompilerParams(
            collective_id=0, has_side_effects=True, vmem_limit_bytes=67043328
        ),
        name="project_gather_attend",
    )(
        span_hidden,
        gain,
        key_value_weight,
        prompt_key_value,
        span_offset,
        cont_lengths,
        cont_query,
        continuation_key_value,
        frequency,
    )
    chunks = 8
    return pl.pallas_call(
        functools.partial(hand_on, chunks),
        out_shape=(
            jax.ShapeDtypeStruct((rows, width), BF16),
            jax.ShapeDtypeStruct((1, tokens, QUERY_HEADS * HEAD_SIZE), BF16),
        ),
        in_specs=[anywhere, anywhere],
        out_specs=(anywhere, anywhere),
        scratch_shapes=[
            pltpu.VMEM((rows, width), BF16),
            pltpu.VMEM((tokens, QUERY_HEADS * HEAD_SIZE), BF16),
            dma((chunks + 1,)),
            dma((chunks + 1,)),
        ],
        compiler_params=pltpu.CompilerParams(vmem_limit_bytes=67043328),
        name="hand_on",
    )(span_rows, attended)


def solution(mesh):
    placed = (
        P("parts", "seq"),
        P("seq"),
        P("seq", "set"),
        P(("parts", "seq"), None),
        P("parts"),
        P(("parts", "set", "seq"), None, None),
        P(("parts", "set", "seq"), None, None),
        P(("parts", "set", "seq")),
    )
    return jax.shard_map(
        functools.partial(on_device, mesh.shape["set"], mesh.shape["seq"]),
        mesh=mesh,
        in_specs=placed,
        out_specs=(P(("parts", "seq"), "set"), P(("parts", "set", "seq"), None, None)),
        check_vma=False,
    )
```

```python
import functools
import math

import jax
import jax.numpy as jnp
import numpy as np
from jax import lax
from jax.experimental import pallas as pl
from jax.experimental.pallas import tpu as pltpu
from jax.sharding import PartitionSpec as P

MODEL_WIDTH = 8192
QUERY_HEADS = 64
KEY_HEADS = 8
HEAD_SIZE = 128
SPAN_LENGTH = 256
GROUP = QUERY_HEADS // KEY_HEADS
KEY_COLUMNS = KEY_HEADS * HEAD_SIZE

EPS = 1e-05
NEGATIVE_LARGE = -1e30
EXPONENT = HEAD_SIZE ** (-0.5) * math.log2(math.e)

MESH = pl.DeviceIdType.MESH
F32 = jnp.float32
BF16 = jnp.bfloat16


def frequency_table():
    index = np.arange(HEAD_SIZE // 2, dtype=np.float64)
    base = 500000.0 ** (-2.0 * index / HEAD_SIZE)
    wave = 2.0 * np.pi / base
    smooth = (8192.0 / wave - 1.0) / 3.0
    blended = (1.0 - smooth) * base / 8.0 + smooth * base
    table = np.where(wave < 2048.0, base, np.where(wave > 8192.0, base / 8.0, blended))
    row = np.concatenate([table, table]).astype(np.float32)
    return np.broadcast_to(row, (8, HEAD_SIZE)).copy()


def rotary_tables(frequency, start, rows):
    positions = (start + lax.broadcasted_iota(jnp.int32, (rows, HEAD_SIZE), 0)).astype(F32)
    angles = positions * frequency
    lane = lax.broadcasted_iota(jnp.int32, (rows, HEAD_SIZE), 1)
    sine = jnp.sin(angles)
    return jnp.cos(angles), jnp.where(lane < HEAD_SIZE // 2, -sine, sine)


def turn(value, cosine, sine):
    return value * cosine + pltpu.roll(value, HEAD_SIZE // 2, 1) * sine


def scores_of(query, keys):
    return lax.dot_general(query, keys, (((1,), (1,)), ((), ())), preferred_element_type=F32)


def with_ones(values):
    return jnp.concatenate([values, jnp.ones_like(values)], axis=1)


def kernel(
    n_set,
    n_seq,
    hidden_hbm,
    gain_hbm,
    weight_hbm,
    prompt_hbm,
    offset_smem,
    length_smem,
    query_hbm,
    own_hbm,
    frequency_hbm,
    span_out,
    attended_out,
    hidden,
    gain,
    weight,
    prompt,
    query_in,
    own,
    frequency,
    scaled,
    partial,
    sending,
    received,
    square_mine,
    square_theirs,
    square_column,
    span,
    query,
    best,
    accum,
    outgoing,
    store_sem,
    load_sem,
    span_store_sem,
    square_send,
    square_recv,
    part_send,
    part_recv,
    pz_send,
    pz_recv,
    px_send,
    px_recv,
    pc_send,
    pc_recv,
    sz_send,
    sz_recv,
    sx_send,
    sx_recv,
    sc_send,
    sc_recv,
):
    n_x = n_set // 2
    me_set = lax.axis_index("set")
    me_seq = lax.axis_index("seq")
    me_x, me_core = me_set // 2, me_set % 2
    width = weight.shape[1]
    rows = span.shape[1] // n_seq
    cached = prompt.shape[1] // n_seq
    tokens = query_in.shape[0]
    halves = 2 if width % 512 == 0 else 1
    half = width // halves

    def seq_at(step):
        return (me_seq + step) % n_seq

    def set_at(step):
        return ((me_x + step) % n_x) * 2 + me_core

    twin = me_x * 2 + 1 - me_core

    def rows_of(which, count):
        return pl.ds(pl.multiple_of(which * count, count), count)

    loads = []

    def load(source, target):
        copy = pltpu.make_async_copy(source, target, load_sem.at[len(loads)])
        copy.start()
        loads.append(copy)
        return copy

    prompt_loads = [
        load(
            prompt_hbm.at[:, pl.ds(s * width, width)],
            prompt.at[s, rows_of(me_seq, cached), :],
        )
        for s in range(n_set)
    ]
    hidden_load = load(hidden_hbm, hidden)
    gain_load = load(gain_hbm, gain)
    weight_loads = [
        load(weight_hbm.at[:, pl.ds(i * half, half)], weight.at[:, pl.ds(i * half, half)])
        for i in range(halves)
    ]

    barrier = pltpu.get_barrier_semaphore()
    partners = [{"seq": seq_at(d)} for d in range(1, n_seq)]
    partners += [{"set": set_at(d)} for d in range(1, n_x)]
    partners += [{"set": twin}]
    for partner in partners:
        pl.semaphore_signal(barrier, inc=1, device_id=partner, device_id_type=MESH)
    for copy in prompt_loads:
        copy.wait()
    pl.semaphore_wait(barrier, len(partners))

    copies = []

    def remote(source, target, send_sem, recv_sem, device):
        return pltpu.make_async_remote_copy(
            src_ref=source,
            dst_ref=target,
            send_sem=send_sem,
            recv_sem=recv_sem,
            device_id=device,
            device_id_type=MESH,
        )

    def send(*args):
        copy = remote(*args)
        copy.start()
        copies.append(copy)
        return copy

    def other_seq(j):
        upper = (2 * me_seq) // n_seq
        low = j + (j - me_seq + n_seq) // n_seq
        down = n_seq - 1 - j
        high = down - (me_seq - down + n_seq) // n_seq
        return low + upper * (high - low)

    others = range(n_seq - 1)

    def prompt_block(s, z):
        return prompt.at[s, rows_of(z, cached), :]

    def span_block(s, i, z):
        return span.at[s * halves + i, rows_of(z, rows), :]

    for j in reversed(others):
        block, z = prompt_block(me_set, me_seq), other_seq(j)
        send(block, block, pz_send.at[z], pz_recv.at[me_seq], {"seq": z})

    hidden_load.wait()
    gain_load.wait()
    squares = jnp.zeros((hidden.shape[0], HEAD_SIZE), F32)
    for i in range(hidden.shape[1] // HEAD_SIZE):
        block = hidden[:, i * HEAD_SIZE : (i + 1) * HEAD_SIZE].astype(F32)
        squares += block * block
        scaled[:, i * HEAD_SIZE : (i + 1) * HEAD_SIZE] = (
            block * gain[i : i + 1, :].astype(F32)
        ).astype(BF16)
    square_row = jnp.sum(squares.T, axis=0, keepdims=True)
    square_mine[...] = jnp.broadcast_to(square_row, square_mine.shape)

    for i in range(halves):
        weight_loads[i].wait()
        if i == 0:
            for j in reversed(others):
                z = other_seq(j)
                send(
                    square_mine,
                    square_theirs.at[me_seq],
                    square_send.at[z],
                    square_recv.at[me_seq],
                    {"seq": z},
                )
        columns = pl.ds(i * half, half)
        product = jnp.dot(scaled[...], weight[:, columns], preferred_element_type=F32)
        partial[:, columns] = product
        sending[i] = product.astype(BF16)
        for j in reversed(others):
            z = other_seq(j)
            send(
                sending.at[i, rows_of(z, rows), :],
                received.at[i, me_seq],
                part_send.at[i, z],
                part_recv.at[i, me_seq],
                {"seq": z},
            )

    own_load = load(own_hbm.at[0], own)
    query_load = load(query_hbm.at[0], query_in)
    frequency_load = load(frequency_hbm, frequency)

    def pass_prompt(j):
        z = other_seq(j)
        block = prompt_block(me_set, z)
        remote(block, block, pz_send.at[z], pz_recv.at[z], {"seq": z}).wait_recv()
        for e in range(1, n_x):
            send(block, block, px_send.at[z, e], px_recv.at[z, e], {"set": set_at(e)})
        send(block, block, pc_send.at[z, 0], pc_recv.at[z, 0], {"set": twin})

    def pass_prompt_twin(j):
        z = other_seq(j)
        for e in range(1, n_x):
            come = prompt_block(set_at(n_x - e), z)
            remote(come, come, px_send.at[z, e], px_recv.at[z, e], {"set": twin}).wait_recv()
            send(come, come, pc_send.at[z, e], pc_recv.at[z, e], {"set": twin})

    frequency_load.wait()
    offset = offset_smem[0]
    cosine, sine = rotary_tables(frequency[0:1, :], offset + SPAN_LENGTH, tokens)
    span_cosine, span_sine = rotary_tables(frequency[0:1, :], offset + me_seq * rows, rows)
    own_load.wait()
    query_load.wait()

    causal = jnp.concatenate(
        [
            lax.broadcasted_iota(jnp.int32, (tokens, tokens), 0)
            >= lax.broadcasted_iota(jnp.int32, (tokens, tokens), 1)
        ]
        * GROUP,
        axis=0,
    )

    def columns_of(head):
        return pl.ds(pl.multiple_of(head * HEAD_SIZE, HEAD_SIZE), HEAD_SIZE)

    def attend_own(head, carry):
        for g in range(GROUP):
            raw = query_in[:, columns_of(head * GROUP + g)].astype(F32)
            query[head, pl.ds(g * tokens, tokens), :] = turn(raw, cosine, sine).astype(BF16)
        keys = turn(own[:, columns_of(head)].astype(F32), cosine, sine).astype(BF16)
        values = own[:, columns_of(head + KEY_HEADS)]
        scores = jnp.where(causal, scores_of(query[head], keys), NEGATIVE_LARGE)
        top = jnp.max(scores, axis=1, keepdims=True)
        weights = jnp.exp2((scores - top) * EXPONENT).astype(BF16)
        best[head] = jnp.broadcast_to(top, best.shape[1:])
        accum[head] = jnp.dot(weights, with_ones(values), preferred_element_type=F32)
        return carry

    lax.fori_loop(0, KEY_HEADS // 4, attend_own, 0)
    for j in others:
        pass_prompt(j)
    lax.fori_loop(KEY_HEADS // 4, KEY_HEADS, attend_own, 0)
    for j in others:
        pass_prompt_twin(j)

    square_total = square_mine[...]
    for j in others:
        z = other_seq(j)
        remote(
            square_mine, square_theirs.at[z], square_send.at[z], square_recv.at[z], {"seq": z}
        ).wait_recv()
        square_total += square_theirs[z]
    square_column[...] = jnp.broadcast_to(
        square_total[0:1, :], (HEAD_SIZE, square_total.shape[1])
    ).T
    inverse = lax.rsqrt(square_column[rows_of(me_seq, rows), :] / MODEL_WIDTH + EPS)

    def finish(i):
        for j in others:
            z = other_seq(j)
            remote(
                sending.at[i, rows_of(z, rows), :],
                received.at[i, z],
                part_send.at[i, z],
                part_recv.at[i, z],
                {"seq": z},
            ).wait_recv()
        for c in range(half // HEAD_SIZE):
            column = i * half + c * HEAD_SIZE
            block = partial[rows_of(me_seq, rows), pl.ds(column, HEAD_SIZE)]
            for j in others:
                block += received[i, other_seq(j), :, pl.ds(c * HEAD_SIZE, HEAD_SIZE)].astype(F32)
            block = block * inverse
            turned = turn(block, span_cosine, span_sine)
            is_key = me_set * width + column < KEY_COLUMNS
            span[
                me_set * halves + i, rows_of(me_seq, rows), pl.ds(c * HEAD_SIZE, HEAD_SIZE)
            ] = jnp.where(is_key, turned, block).astype(BF16)
        mine = span_block(me_set, i, me_seq)
        for e in range(1, n_x):
            send(
                mine, mine, sx_send.at[i, me_seq, e], sx_recv.at[i, me_seq, e], {"set": set_at(e)}
            )
        for j in others:
            z = other_seq(j)
            send(mine, mine, sz_send.at[i, z], sz_recv.at[i, me_seq], {"seq": z})
        send(mine, mine, sc_send.at[i, me_seq, 0], sc_recv.at[i, me_seq, 0], {"set": twin})
        span_store(i).start()

    def span_store(i):
        return pltpu.make_async_copy(
            span_block(me_set, i, me_seq),
            span_out.at[:, pl.ds(i * half, half)],
            span_store_sem.at[i],
        )

    def pass_span(i, j):
        z = other_seq(j)
        block = span_block(me_set, i, z)
        remote(block, block, sz_send.at[i, z], sz_recv.at[i, z], {"seq": z}).wait_recv()
        for e in range(1, n_x):
            send(block, block, sx_send.at[i, z, e], sx_recv.at[i, z, e], {"set": set_at(e)})
        send(block, block, sc_send.at[i, z, 0], sc_recv.at[i, z, 0], {"set": twin})

    def pass_span_twin(i, z):
        for e in range(1, n_x):
            come = span_block(set_at(n_x - e), i, z)
            remote(
                come, come, sx_send.at[i, z, e], sx_recv.at[i, z, e], {"set": twin}
            ).wait_recv()
            send(come, come, sc_send.at[i, z, e], sc_recv.at[i, z, e], {"set": twin})

    def span_arrived(i):
        twin_x = twin
        for z in range(n_seq):
            for e in range(n_x):
                come = span_block(twin_x, i, z)
                remote(
                    come, come, sc_send.at[i, z, e], sc_recv.at[i, z, e], {"set": twin}
                ).wait_recv()

    def attend_more(head, keys, values, mask):
        scores = scores_of(query[head], keys)
        if mask is not None:
            scores = jnp.where(mask, scores, NEGATIVE_LARGE)
        old = best[head]
        top = jnp.maximum(old, jnp.max(scores, axis=1, keepdims=True))
        spread = jnp.concatenate([top] * (scores.shape[1] // HEAD_SIZE), axis=1)
        weights = jnp.exp2((scores - spread) * EXPONENT).astype(BF16)
        shrink = jnp.exp2((old - top) * EXPONENT)
        total = accum[head] * jnp.concatenate([shrink, shrink], axis=1) + jnp.dot(
            weights, with_ones(values), preferred_element_type=F32
        )
        return top, total

    kept = lax.broadcasted_iota(jnp.int32, (tokens, HEAD_SIZE), 0) < length_smem[0]
    per_set = width // HEAD_SIZE
    per_part = half // HEAD_SIZE
    live = lax.broadcasted_iota(jnp.int32, (1, prompt.shape[1]), 1) < offset

    def prompt_head(head):
        return prompt[head // per_set, :, columns_of(head % per_set)]

    def span_head(head):
        start = head % per_part * HEAD_SIZE
        return span[head // per_part, :, start : start + HEAD_SIZE]

    def attend_prompt(head, carry):
        top, total = attend_more(head, prompt_head(head), prompt_head(head + KEY_HEADS), live)
        best[head] = top
        accum[head] = total
        return carry

    def store_of(head):
        columns = pl.ds(head * GROUP * HEAD_SIZE, GROUP * HEAD_SIZE)
        return pltpu.make_async_copy(
            outgoing.at[:, columns], attended_out.at[:, columns], store_sem.at[head]
        )

    def attend_span(head):
        top, total = attend_more(head, span_head(head), span_head(head + KEY_HEADS), None)
        mixed = total[:, :HEAD_SIZE] / total[:, HEAD_SIZE:]
        for g in range(GROUP):
            column = (head * GROUP + g) * HEAD_SIZE
            outgoing[:, column : column + HEAD_SIZE] = jnp.where(
                kept, mixed[g * tokens : (g + 1) * tokens, :], 0.0
            ).astype(BF16)
        store_of(head).start()

    def prompt_arrived():
        for j in others:
            z = other_seq(j)
            for e in range(n_x):
                come = prompt_block(twin, z)
                remote(
                    come, come, pc_send.at[z, e], pc_recv.at[z, e], {"set": twin}
                ).wait_recv()

    finish(0)
    prompt_arrived()
    middle = KEY_HEADS // 2
    lax.fori_loop(0, middle, attend_prompt, 0)
    for i in range(1, halves):
        finish(i)
    pass_span_twin(0, me_seq)
    for j in others:
        pass_span(0, j)
        cut = [middle + (KEY_HEADS - middle) * k // (n_seq - 1) for k in (j, j + 1)]
        if cut[0] < cut[1]:
            lax.fori_loop(cut[0], cut[1], attend_prompt, 0)
    for j in others:
        pass_span_twin(0, other_seq(j))
    for i in range(halves):
        heads = [h for h in range(KEY_HEADS) if h % per_set // per_part == i]
        steps = []
        if i + 1 < halves:
            steps = [functools.partial(pass_span_twin, i + 1, me_seq)]
            steps += [functools.partial(pass_span, i + 1, j) for j in others]
        for step in steps[:2]:
            step()
        span_arrived(i)
        for k, head in enumerate(heads):
            attend_span(head)
            if 2 + k < len(steps):
                steps[2 + k]()
        for step in steps[2 + len(heads) :]:
            step()
        if i + 1 < halves:
            for j in others:
                pass_span_twin(i + 1, other_seq(j))

    for copy in copies:
        copy.wait_send()
    for i in range(halves):
        span_store(i).wait()
    for head in range(KEY_HEADS):
        store_of(head).wait()


def hand_on(chunks, span_in, attended_in, span_out, attended_out, rows, tokens, in_sem, out_sem):
    step = tokens.shape[0] // chunks
    parts = [pl.ds(c * step, step) for c in range(chunks)]
    ins = [
        pltpu.make_async_copy(attended_in.at[part, :], tokens.at[part, :], in_sem.at[c])
        for c, part in enumerate(parts)
    ] + [pltpu.make_async_copy(span_in, rows, in_sem.at[chunks])]
    outs = [
        pltpu.make_async_copy(tokens.at[part, :], attended_out.at[0, part, :], out_sem.at[c])
        for c, part in enumerate(parts)
    ] + [pltpu.make_async_copy(rows, span_out, out_sem.at[chunks])]
    for copy in ins:
        copy.start()
    for arriving, leaving in zip(ins, outs):
        arriving.wait()
        leaving.start()
    for copy in outs:
        copy.wait()


def on_device(
    n_set,
    n_seq,
    span_hidden,
    norm_gain,
    key_value_weight,
    prompt_key_value,
    span_offset,
    cont_query,
    continuation_key_value,
    cont_lengths,
):
    span_length, features = span_hidden.shape
    width = key_value_weight.shape[1]
    rows = span_length // n_seq
    cached = prompt_key_value.shape[0]
    tokens = cont_query.shape[1]
    n_x = n_set // 2
    halves = 2 if width % 512 == 0 else 1
    half = width // halves
    frequency = jnp.asarray(frequency_table())
    gain = norm_gain.reshape(features // HEAD_SIZE, HEAD_SIZE)
    dma = pltpu.SemaphoreType.DMA
    anywhere = pl.BlockSpec(memory_space=pl.ANY)
    span_rows, attended = pl.pallas_call(
        functools.partial(kernel, n_set, n_seq),
        out_shape=(
            jax.ShapeDtypeStruct((rows, width), BF16),
            jax.ShapeDtypeStruct((tokens, QUERY_HEADS * HEAD_SIZE), BF16),
        ),
        in_specs=[
            anywhere,
            anywhere,
            anywhere,
            anywhere,
            pl.BlockSpec(memory_space=pltpu.SMEM),
            pl.BlockSpec(memory_space=pltpu.SMEM),
            anywhere,
            anywhere,
            anywhere,
        ],
        out_specs=(anywhere, anywhere),
        scratch_shapes=[
            pltpu.VMEM((span_length, features), BF16),
            pltpu.VMEM((features // HEAD_SIZE, HEAD_SIZE), BF16),
            pltpu.VMEM((features, width), BF16),
            pltpu.VMEM((n_set, cached * n_seq, width), BF16),
            pltpu.VMEM((tokens, QUERY_HEADS * HEAD_SIZE), BF16),
            pltpu.VMEM((tokens, 2 * KEY_COLUMNS), BF16),
            pltpu.VMEM((8, HEAD_SIZE), F32),
            pltpu.VMEM((span_length, features), BF16),
            pltpu.VMEM((span_length, width), F32),
            pltpu.VMEM((halves, span_length, half), BF16),
            pltpu.VMEM((halves, n_seq, rows, half), BF16),
            pltpu.VMEM((8, span_length), F32),
            pltpu.VMEM((n_seq, 8, span_length), F32),
            pltpu.VMEM((span_length, HEAD_SIZE), F32),
            pltpu.VMEM((n_set * halves, span_length, half), BF16),
            pltpu.VMEM((KEY_HEADS, GROUP * tokens, HEAD_SIZE), BF16),
            pltpu.VMEM((KEY_HEADS, GROUP * tokens, HEAD_SIZE), F32),
            pltpu.VMEM((KEY_HEADS, GROUP * tokens, 2 * HEAD_SIZE), F32),
            pltpu.VMEM((tokens, QUERY_HEADS * HEAD_SIZE), BF16),
            dma((KEY_HEADS,)),
            dma((n_set + halves + 5,)),
            dma((halves,)),
            dma((n_seq,)),
            dma((n_seq,)),
            dma((halves, n_seq)),
            dma((halves, n_seq)),
            dma((n_seq,)),
            dma((n_seq,)),
            dma((n_seq, n_x)),
            dma((n_seq, n_x)),
            dma((n_seq, n_x)),
            dma((n_seq, n_x)),
            dma((halves, n_seq)),
            dma((halves, n_seq)),
            dma((halves, n_seq, n_x)),
            dma((halves, n_seq, n_x)),
            dma((halves, n_seq, n_x)),
            dma((halves, n_seq, n_x)),
        ],
        compiler_params=pltpu.CompilerParams(
            collective_id=0, has_side_effects=True, vmem_limit_bytes=67043328
        ),
        name="project_gather_attend",
    )(
        span_hidden,
        gain,
        key_value_weight,
        prompt_key_value,
        span_offset,
        cont_lengths,
        cont_query,
        continuation_key_value,
        frequency,
    )
    chunks = 8
    return pl.pallas_call(
        functools.partial(hand_on, chunks),
        out_shape=(
            jax.ShapeDtypeStruct((rows, width), BF16),
            jax.ShapeDtypeStruct((1, tokens, QUERY_HEADS * HEAD_SIZE), BF16),
        ),
        in_specs=[anywhere, anywhere],
        out_specs=(anywhere, anywhere),
        scratch_shapes=[
            pltpu.VMEM((rows, width), BF16),
            pltpu.VMEM((tokens, QUERY_HEADS * HEAD_SIZE), BF16),
            dma((chunks + 1,)),
            dma((chunks + 1,)),
        ],
        compiler_params=pltpu.CompilerParams(vmem_limit_bytes=67043328),
        name="hand_on",
    )(span_rows, attended)


def solution(mesh):
    placed = (
        P("parts", "seq"),
        P("seq"),
        P("seq", "set"),
        P(("parts", "seq"), None),
        P("parts"),
        P(("parts", "set", "seq"), None, None),
        P(("parts", "set", "seq"), None, None),
        P(("parts", "set", "seq")),
    )
    return jax.shard_map(
        functools.partial(on_device, mesh.shape["set"], mesh.shape["seq"]),
        mesh=mesh,
        in_specs=placed,
        out_specs=(P(("parts", "seq"), "set"), P(("parts", "set", "seq"), None, None)),
        check_vma=False,
    )
```
